32 devices in a mesh: range: 4 (over y, core), chan: 8 (over z, x).
Axes of the slice: x: 2, y: 2, z: 4, core: 2. Of those that a mesh axis runs over, the one named last changes fastest.
Arguments:
- echoes: float32 [2, 64, 512, 1024], P(None, 'chan', None, 'range'), may hold values from -18 to 18
- chirp: float32 [2, 129], replicated, may hold values from -0.375 to 0.375
- train_mask: int32 [512, 8], P('chan', 'range'), may hold values from 0 to 1, as said below
Outputs:
- spectra: bfloat16 [2, 512, 64, 1024], P(None, 'chan', None, 'range')
- factors: float32 [512, 2, 128, 128], P('chan')
The draws below stay inside these ranges and needn't reach their ends.
Inputs may be any that keep to these rules, and one draw needn't show every extreme that they name: `train_mask`: in each Doppler bin exactly 4 consecutive tiles are 0 and all other tiles are 1.
All inputs are finite; a program needn't handle non-finite values.
Results may differ from the reference program's by a relative error of at most 0.001.
Values sent between devices are 32-bit elements; how exact they have to be, the bound alone decides.
A program may use at most 128 MiB of HBM per device.

```python
import math
import jax
import jax.numpy as jnp
from jax import lax

CH = 64
PULSES = 512
TAPS = 129
TILE = 128
EXCL = 4
GATES = 1024
NTILES = 8


def draw_echoes(key, part):
    noise_key, level_key = jax.random.split(key)
    levels = jnp.exp(jax.random.uniform(level_key, (NTILES,), jnp.float32, math.log(0.3), math.log(3.0)))
    noise_draw = jnp.clip(jax.random.normal(noise_key, (2, CH, PULSES, GATES), jnp.float32), -6.0, 6.0)
    profile = jnp.broadcast_to(levels[:, None], (NTILES, TILE)).reshape(GATES)
    return noise_draw * profile


def draw_train_mask(key, part):
    starts = jax.random.randint(key, (PULSES, 1), 0, NTILES - EXCL + 1)
    tile_index = jnp.arange(NTILES, dtype=jnp.int32)[None, :]
    inside = (tile_index >= starts) & (tile_index < starts + EXCL)
    return jnp.where(inside, 0, 1).astype(jnp.int32)


def centred(key, extent, spread, reach, held_as=jnp.bfloat16):
    array = jax.random.normal(key, extent, jnp.float32) * spread
    return jnp.minimum(jnp.maximum(array, -reach), reach).astype(held_as)


def setup_inputs(seed: int = 0) -> dict:
    splits = jax.random.split(jax.random.key(seed), 4)
    echoes = draw_echoes(jax.random.fold_in(splits[3], 71), 0)
    chirp = centred(splits[1], (2, TAPS), (2 * TAPS) ** -0.5, 0.375, jnp.float32)
    train_mask = draw_train_mask(jax.random.fold_in(splits[3], 71), 0)
    return {"echoes": echoes, "chirp": chirp, "train_mask": train_mask}


best_precision = lax.Precision.HIGHEST

def toeplitz_rows(taps):
    tap_span = taps.shape[-1] - 1
    padded = jnp.concatenate([taps, jnp.zeros((taps.shape[0], tap_span), taps.dtype)], -1)
    tiled = jnp.tile(padded, (1, tap_span))
    return tiled[:, :2 * tap_span * tap_span].reshape(taps.shape[0], tap_span, 2 * tap_span)

def compress(extended, taps):
    tap_span = taps.shape[-1] - 1
    lead_shape = extended.shape[:-1]
    block_count = extended.shape[-1] // tap_span - 1
    blocks = extended.reshape(lead_shape + (block_count + 1, tap_span))
    window = jnp.concatenate([blocks[..., :block_count, :], blocks[..., 1:, :]], -1)
    kernel = toeplitz_rows(taps)
    products = jnp.einsum('tcpnk,sok->tscpno', window, kernel, precision=best_precision, preferred_element_type=jnp.float32)
    real_part = products[0, 0] + products[1, 1]
    imag_part = products[1, 0] - products[0, 1]
    return jnp.stack([real_part, imag_part]).reshape(lead_shape + (block_count * tap_span,))

def doppler_table(bin_numbers, pulse_count):
    phase_index = bin_numbers[:, None] * jnp.arange(pulse_count, dtype=jnp.int32)[None, :] % pulse_count
    angles = phase_index.astype(jnp.float32) * (2.0 * math.pi / pulse_count)
    scaling = 1.0 / math.sqrt(pulse_count)
    return jnp.stack([jnp.cos(angles) * scaling, -jnp.sin(angles) * scaling])

def doppler(signal, dft_table):
    products = jnp.einsum('sdp,tcpg->stdcg', dft_table, signal, precision=best_precision, preferred_element_type=jnp.float32)
    return jnp.stack([products[0, 0] - products[1, 1], products[0, 1] + products[1, 0]])

def gram_block(spectra_now, spectra_next, weights, scaling):
    snapshot = jnp.concatenate([spectra_now, spectra_next], 2)
    masked = snapshot * weights[None, :, None, :]
    products = jnp.einsum('tbkg,sblg->btskl', masked, snapshot, precision=best_precision, preferred_element_type=jnp.float32)
    real_part = products[:, 0, 0] + products[:, 1, 1]
    imag_part = products[:, 0, 1] - products[:, 1, 0]
    return jnp.stack([real_part, imag_part], 1) * scaling

def factor(gram):
    order_size = gram.shape[-1]
    strip_size = min(16, order_size)
    columns = jnp.arange(order_size, dtype=jnp.int32)
    remaining = gram
    pieces = []
    for offset in range(0, order_size, strip_size):
        strip_rows = remaining[:, :, :strip_size, :]

        def column_step(position, carry):
            strip_now, found_rows = carry
            place = offset + position
            row_now = lax.dynamic_index_in_dim(strip_now, position, 2, keepdims=False)
            pivots = lax.optimization_barrier(jnp.sum(jnp.where(columns == place, row_now[:, 0], 0.0), -1))
            inverse = lax.rsqrt(pivots)[:, None]
            row_real = jnp.where(columns >= place, row_now[:, 0] * inverse, 0.0)
            row_imag = jnp.where(columns > place, row_now[:, 1] * inverse, 0.0)
            coef_real = row_real[:, offset:offset + strip_size]
            coef_imag = row_imag[:, offset:offset + strip_size]
            new_real = strip_now[:, 0] - coef_real[:, :, None] * row_real[:, None, :] - coef_imag[:, :, None] * row_imag[:, None, :]
            new_imag = strip_now[:, 1] - coef_real[:, :, None] * row_imag[:, None, :] + coef_imag[:, :, None] * row_real[:, None, :]
            found_rows = lax.dynamic_update_index_in_dim(found_rows, jnp.stack([row_real, row_imag], 1), position, 2)
            return (jnp.stack([new_real, new_imag], 1), found_rows)
        strip_end, found_rows = lax.fori_loop(0, strip_size, column_step, (strip_rows, jnp.zeros_like(strip_rows)))
        pieces.append(found_rows)
        if offset + strip_size < order_size:
            tail_part = found_rows[:, :, :, offset + strip_size:]
            products = jnp.einsum('nabi,ncbj->nacij', tail_part, found_rows, precision=best_precision, preferred_element_type=jnp.float32)
            update_real = products[:, 0, 0] + products[:, 1, 1]
            update_imag = products[:, 0, 1] - products[:, 1, 0]
            remaining = remaining[:, :, strip_size:, :] - jnp.stack([update_real, update_imag], 1)
    return jnp.concatenate(pieces, 2)

def reference(echoes, chirp, train_mask):
    tap_span = TAPS - 1
    dft_table = doppler_table(jnp.arange(PULSES, dtype=jnp.int32), PULSES)

    def per_channel(channel_index):
        channel_data = lax.dynamic_index_in_dim(echoes, channel_index, 1, keepdims=False)
        padded = jnp.concatenate([channel_data, jnp.zeros((2, PULSES, tap_span), channel_data.dtype)], -1)
        compressed = compress(padded[:, None], chirp)
        return doppler(compressed, dft_table)[:, :, 0]
    per_chan = lax.map(per_channel, jnp.arange(CH, dtype=jnp.int32))
    spectra_full = jnp.moveaxis(per_chan, 0, 2)
    weights = jnp.broadcast_to(train_mask.astype(jnp.float32)[:, :, None], (PULSES, NTILES, TILE)).reshape(PULSES, GATES)
    scaling = 1.0 / GATES

    def per_bin(bin_index):
        bin_now = lax.dynamic_slice_in_dim(spectra_full, bin_index, 1, 1)
        bin_after = lax.dynamic_slice_in_dim(spectra_full, (bin_index + 1) % PULSES, 1, 1)
        return gram_block(bin_now, bin_after, lax.dynamic_slice_in_dim(weights, bin_index, 1, 0), scaling)[0]
    gram_all = lax.map(per_bin, jnp.arange(PULSES, dtype=jnp.int32))
    factors = factor(gram_all)
    return (spectra_full.astype(jnp.bfloat16), factors)
```

```python
import functools
import math

import jax
import jax.numpy as jnp
from jax import lax
from jax.experimental import pallas as pl
from jax.experimental.pallas import tpu as pltpu
from jax.sharding import PartitionSpec as P

LANES = 128
STRIP = 16
BF = jnp.bfloat16
F32 = jnp.float32
VMEM_LIMIT = 60 * 1024 * 1024


def split(x):
    high = x.astype(BF)
    return high, (x - high.astype(F32)).astype(BF)


def split_table(x):
    high = lax.reduce_precision(x, 8, 7)
    return high.astype(BF), (x - high).astype(BF)


def dot(a, b, dims=((1,), (0,))):
    return lax.dot_general(a, b, (dims, ((), ())), preferred_element_type=F32)


def dot3(a, b, dims=((1,), (0,))):
    (ah, al), (bh, bl) = a, b
    return dot(ah, bh, dims) + (dot(ah, bl, dims) + dot(al, bh, dims))


def from_behind(value, axis, steps):
    count = lax.axis_size(axis)
    leading, last = (max(0, -steps), min(count, count - steps))
    return lax.ppermute(value, axis, [(s, s + steps) for s in range(leading, last)])


def from_behind_2(block, axis, distance):
    devices = range(lax.axis_size(axis))
    route = [((i - distance) % len(devices), i) for i in devices]
    return lax.ppermute(block, axis, route)


def toeplitz_rows(taps):
    tap_span = taps.shape[-1] - 1
    padded = jnp.concatenate([taps, jnp.zeros((taps.shape[0], tap_span), taps.dtype)], -1)
    tiled = jnp.tile(padded, (1, tap_span))
    return tiled[:, : 2 * tap_span * tap_span].reshape(taps.shape[0], tap_span, 2 * tap_span)


def doppler_table(pulses):
    bins = jnp.arange(pulses, dtype=jnp.int32)
    phase = bins[:, None] * bins[None, :] % pulses
    angles = phase.astype(F32) * (2.0 * math.pi / pulses)
    scaling = 1.0 / math.sqrt(pulses)
    return jnp.concatenate([jnp.cos(angles) * scaling, -jnp.sin(angles) * scaling])


def spectra_kernel(channels, pulses, tiles, e_ref, h_ref, kh_ref, kl_ref, th_ref, tl_ref, s_ref):
    channel = pl.program_id(0)
    kernel = (kh_ref[...], kl_ref[...])
    wide = [jnp.concatenate([e_ref[p, 0], h_ref[p, 0]], -1) for p in range(2)]
    for t in range(tiles):
        window = jnp.concatenate(
            [w[:, t * LANES : (t + 2) * LANES] for w in wide], -1
        )
        y = split(dot3(split(window), kernel))
        step = min(256, pulses)
        for b in range(0, pulses, step):
            re = dot3((th_ref[pl.ds(b, step), :], tl_ref[pl.ds(b, step), :]), y)
            im = dot3((th_ref[pl.ds(pulses + b, step), :], tl_ref[pl.ds(pulses + b, step), :]), y)
            rows = pl.ds(b * channels + channel, step, stride=channels)
            s_ref[0, t, rows, :] = re[:, :LANES] - im[:, LANES:]
            s_ref[1, t, rows, :] = re[:, LANES:] + im[:, :LANES]


def make_spectra(echoes, rim, chirp):
    _, channels, pulses, gates = echoes.shape
    tiles = gates // LANES
    rows = toeplitz_rows(chirp)
    kr, ki = rows[0].T, rows[1].T
    kernel = jnp.concatenate(
        [jnp.concatenate([kr, -ki], 1), jnp.concatenate([ki, kr], 1)], 0
    )
    kh, kl = split_table(kernel)
    th, tl = split_table(doppler_table(pulses))
    full = lambda a: pl.BlockSpec(a.shape, lambda c: (0,) * a.ndim, pipeline_mode=pl.Buffered(1))
    return pl.pallas_call(
        functools.partial(spectra_kernel, channels, pulses, tiles),
        grid=(channels,),
        in_specs=[
            pl.BlockSpec((2, 1, pulses, gates), lambda c: (0, c, 0, 0)),
            pl.BlockSpec((2, 1, pulses, LANES), lambda c: (0, c, 0, 0)),
            full(kh), full(kl), full(th), full(tl),
        ],
        out_specs=pl.BlockSpec((2, tiles, pulses * channels, LANES), lambda c: (0, 0, 0, 0)),
        out_shape=jax.ShapeDtypeStruct((2, tiles, pulses * channels, LANES), F32),
        compiler_params=pltpu.CompilerParams(vmem_limit_bytes=VMEM_LIMIT),
        name="spectra",
    )(echoes, rim, kh, kl, th, tl)


def gram_kernel(bins, channels, tiles, scaling, w_ref, r_ref, f_ref, z_ref, o_ref):
    first = pl.program_id(0) * bins
    order = 2 * channels
    rows = lax.broadcasted_iota(jnp.int32, (order, order), 0)
    cols = lax.broadcasted_iota(jnp.int32, (order, order), 1)
    upper = rows <= cols

    def parts(j, part, t):
        now = r_ref[part, t, j]
        after = r_ref[part, t, j + 1] if j + 1 < bins else f_ref[part, t, 0]
        return jnp.concatenate([now, after], 0)

    for j in range(bins):
        pieces = [[parts(j, part, t) for t in range(tiles)] for part in range(2)]
        whole = jnp.concatenate([jnp.concatenate(p, 1) for p in pieces], 0)
        masked = jnp.concatenate(
            [
                jnp.concatenate(
                    [pieces[part][t] * w_ref[first + j, t] for t in range(tiles)], 1
                )
                for part in range(2)
            ],
            0,
        )
        g = dot3(split(masked), split(whole), ((1,), (1,)))
        re = g[:order, :order] + g[order:, order:]
        im = g[:order, order:] - g[order:, :order]
        z_ref[j] = jnp.where(upper, re, im) * scaling
        for part in range(2):
            for t in range(tiles):
                o_ref[part, j, :, t * LANES : (t + 1) * LANES] = r_ref[part, t, j].astype(BF)


def make_gram(turned, firsts, weights, scaling, bins):
    _, tiles, total, channels, _ = turned.shape
    order = 2 * channels
    return pl.pallas_call(
        functools.partial(gram_kernel, bins, channels, tiles, scaling),
        grid=(total // bins,),
        in_specs=[
            pl.BlockSpec(memory_space=pltpu.SMEM),
            pl.BlockSpec((2, tiles, bins, channels, LANES), lambda i: (0, 0, i, 0, 0)),
            pl.BlockSpec((2, tiles, 1, channels, LANES), lambda i: (0, 0, i, 0, 0)),
        ],
        out_specs=[
            pl.BlockSpec((bins, order, order), lambda i: (i, 0, 0)),
            pl.BlockSpec((2, bins, channels, tiles * LANES), lambda i: (0, i, 0, 0)),
        ],
        out_shape=[
            jax.ShapeDtypeStruct((total, order, order), F32),
            jax.ShapeDtypeStruct((2, total, channels, tiles * LANES), BF),
        ],
        compiler_params=pltpu.CompilerParams(vmem_limit_bytes=VMEM_LIMIT),
        name="gram",
    )(weights, turned, firsts)


def factor_kernel(count, order, z_ref, o_ref, re_ref, im_ref, sr_ref, si_ref):
    rows = lax.broadcasted_iota(jnp.int32, (order, order), 0)
    cols = lax.broadcasted_iota(jnp.int32, (order, order), 1)
    lane = lax.broadcasted_iota(jnp.int32, (count, order), 1)

    @pl.loop(0, count)
    def _(b):
        z = z_ref[b]
        re_ref[b] = z
        im_ref[b] = jnp.where(rows < cols, -z.T, 0.0)

    for offset in range(0, order, STRIP):
        for b in range(count):
            sr_ref[pl.ds(b, STRIP, stride=count), :] = re_ref[b, offset : offset + STRIP, :]
            si_ref[pl.ds(b, STRIP, stride=count), :] = im_ref[b, offset : offset + STRIP, :]
        now_r = [sr_ref[i * count : (i + 1) * count, :] for i in range(STRIP)]
        now_i = [si_ref[i * count : (i + 1) * count, :] for i in range(STRIP)]
        for i in range(STRIP):
            k = offset + i
            pivot = jnp.broadcast_to(now_r[i][:, k : k + 1], (count, order))
            root = lax.rsqrt(pivot)
            row_r = jnp.where(lane >= k, now_r[i] * root, 0.0)
            row_i = jnp.where(lane > k, now_i[i] * root, 0.0)
            for j in range(i + 1, STRIP):
                m = offset + j
                cr = jnp.broadcast_to(row_r[:, m : m + 1], (count, order))
                ci = jnp.broadcast_to(row_i[:, m : m + 1], (count, order))
                now_r[j] = now_r[j] - cr * row_r - ci * row_i
                now_i[j] = now_i[j] - cr * row_i + ci * row_r
            sr_ref[i * count : (i + 1) * count, :] = row_r
            si_ref[i * count : (i + 1) * count, :] = row_i
        done = offset + STRIP

        for b in range(count):
            fr = sr_ref[pl.ds(b, STRIP, stride=count), :]
            fi = si_ref[pl.ds(b, STRIP, stride=count), :]
            o_ref[b, 0, offset:done, :] = fr
            o_ref[b, 1, offset:done, :] = fi
            if done < order:
                left = jnp.concatenate([fr, fi], 0)
                right = jnp.concatenate(
                    [jnp.concatenate([fr, fi], 0), jnp.concatenate([fi, -fr], 0)], 1
                )
                lh, ll = split(left)
                rh, rl = split(right)
                update = dot(
                    jnp.concatenate([lh, lh, ll], 0)[:, :],
                    jnp.concatenate([rh, rl, rh], 0),
                    ((0,), (0,)),
                )
                re_ref[b, done:, :] = re_ref[b, done:, :] - update[done:, :order]
                im_ref[b, done:, :] = im_ref[b, done:, :] - update[done:, order:]


def make_factor(gram):
    count, order, _ = gram.shape
    return pl.pallas_call(
        functools.partial(factor_kernel, count, order),
        out_shape=jax.ShapeDtypeStruct((count, 2, order, order), F32),
        scratch_shapes=[
            pltpu.VMEM((count, order, order), F32),
            pltpu.VMEM((count, order, order), F32),
            pltpu.VMEM((STRIP * count, order), F32),
            pltpu.VMEM((STRIP * count, order), F32),
        ],
        compiler_params=pltpu.CompilerParams(vmem_limit_bytes=VMEM_LIMIT),
        name="factor",
    )(gram)


def pack_factor(factors):
    order = factors.shape[-1]
    keep = jnp.arange(order)[:, None] <= jnp.arange(order)[None, :]
    return jnp.where(keep, factors[:, 0], jnp.swapaxes(factors[:, 1], 1, 2))


def unpack_kernel(p_ref, o_ref):
    order = p_ref.shape[-1]
    rows = lax.broadcasted_iota(jnp.int32, (order, order), 0)
    cols = lax.broadcasted_iota(jnp.int32, (order, order), 1)
    for b in range(p_ref.shape[0]):
        z = p_ref[b]
        o_ref[b, 0] = jnp.where(rows <= cols, z, 0.0)
        o_ref[b, 1] = jnp.where(rows < cols, z.T, 0.0)


def unpack_factor(packed):
    total, order, _ = packed.shape
    bins = math.gcd(total, 8)
    return pl.pallas_call(
        unpack_kernel,
        grid=(total // bins,),
        in_specs=[pl.BlockSpec((bins, order, order), lambda i: (i, 0, 0))],
        out_specs=pl.BlockSpec((bins, 2, order, order), lambda i: (i, 0, 0, 0)),
        out_shape=jax.ShapeDtypeStruct((total, 2, order, order), F32),
        name="unpack",
    )(packed)


def on_device(echoes, chirp, train_mask):
    tap_span = chirp.shape[-1] - 1
    _, channels, pulses, gates = echoes.shape
    tiles = gates // LANES
    rim = from_behind(echoes[..., :tap_span], "range", -1)
    spectra = make_spectra(echoes, rim, chirp)
    spectra = spectra.reshape(2, tiles, pulses, channels, LANES)
    turned = lax.all_to_all(spectra, "chan", split_axis=2, concat_axis=3, tiled=True)
    edge = from_behind_2(turned[:, :, :1], "chan", -1)
    bins = math.gcd(turned.shape[2], 8)
    firsts = jnp.concatenate([turned[:, :, bins::bins], edge], 2)
    scaling = 1.0 / (gates * lax.axis_size("range"))
    packed, spectra_out = make_gram(turned, firsts, train_mask.astype(F32), scaling, bins)
    share = lax.psum_scatter(packed, "range", scatter_dimension=0, tiled=True)
    mine = pack_factor(make_factor(share))
    factors = unpack_factor(lax.all_gather(mine, "range", axis=0, tiled=True))
    return (spectra_out, factors)


def solution(mesh):
    return jax.shard_map(
        on_device,
        mesh=mesh,
        in_specs=(P(None, "chan", None, "range"), P(), P("chan", "range")),
        out_specs=(P(None, "chan", None, "range"), P("chan", None, None, None)),
        check_vma=False,
    )
```

```python
import functools
import math

import jax
import jax.numpy as jnp
from jax import lax
from jax.experimental import pallas as pl
from jax.experimental.pallas import tpu as pltpu
from jax.sharding import PartitionSpec as P

LANES = 128
STRIP = 16
CHUNKS = 4
BF = jnp.bfloat16
F32 = jnp.float32
VMEM_LIMIT = 60 * 1024 * 1024


def split(x):
    high = x.astype(BF)
    return high, (x - high.astype(F32)).astype(BF)


def split_table(x):
    high = lax.reduce_precision(x, 8, 7)
    return high.astype(BF), (x - high).astype(BF)


def dot(a, b, dims=((1,), (0,))):
    return lax.dot_general(a, b, (dims, ((), ())), preferred_element_type=F32)


def dot3(a, b, dims=((1,), (0,))):
    (ah, al), (bh, bl) = a, b
    return dot(ah, bh, dims) + (dot(ah, bl, dims) + dot(al, bh, dims))


def from_behind(value, axis, steps):
    count = lax.axis_size(axis)
    leading, last = (max(0, -steps), min(count, count - steps))
    return lax.ppermute(value, axis, [(s, s + steps) for s in range(leading, last)])


def from_behind_2(block, axis, distance):
    devices = range(lax.axis_size(axis))
    route = [((i - distance) % len(devices), i) for i in devices]
    return lax.ppermute(block, axis, route)


def toeplitz_rows(taps):
    tap_span = taps.shape[-1] - 1
    padded = jnp.concatenate([taps, jnp.zeros((taps.shape[0], tap_span), taps.dtype)], -1)
    tiled = jnp.tile(padded, (1, tap_span))
    return tiled[:, : 2 * tap_span * tap_span].reshape(taps.shape[0], tap_span, 2 * tap_span)


def doppler_table(pulses):
    bins = jnp.arange(pulses, dtype=jnp.int32)
    phase = bins[:, None] * bins[None, :] % pulses
    angles = phase.astype(F32) * (2.0 * math.pi / pulses)
    scaling = 1.0 / math.sqrt(pulses)
    return jnp.concatenate([jnp.cos(angles) * scaling, -jnp.sin(angles) * scaling])


def spectra_kernel(channels, pulses, tiles, wrap, e_ref, h_ref, kh_ref, kl_ref, th_ref, tl_ref, s_ref):
    channel = pl.program_id(0)
    kernel = (kh_ref[...], kl_ref[...])
    wide = [jnp.concatenate([e_ref[p, 0], h_ref[p, 0]], -1) for p in range(2)]
    for t in range(tiles):
        window = jnp.concatenate(
            [w[:, t * LANES : (t + 2) * LANES] for w in wide], -1
        )
        y = split(dot3(split(window), kernel))
        step = min(256, pulses)
        for b in range(0, pulses, step):
            re = dot3((th_ref[pl.ds(b, step), :], tl_ref[pl.ds(b, step), :]), y)
            im = dot3((th_ref[pl.ds(pulses + b, step), :], tl_ref[pl.ds(pulses + b, step), :]), y)
            rows = pl.ds(b * channels + channel, step, stride=channels)
            real = re[:, :LANES] - im[:, LANES:]
            imag = re[:, LANES:] + im[:, :LANES]
            s_ref[0, t, rows, :] = real
            s_ref[1, t, rows, :] = imag
            if wrap and b == 0:
                s_ref[0, t, pl.ds(pulses * channels + channel, 1), :] = real[:1]
                s_ref[1, t, pl.ds(pulses * channels + channel, 1), :] = imag[:1]


def make_spectra(echoes, rim, chirp, wrap):
    _, channels, pulses, gates = echoes.shape
    tiles = gates // LANES
    rows = toeplitz_rows(chirp)
    kr, ki = rows[0].T, rows[1].T
    kernel = jnp.concatenate(
        [jnp.concatenate([kr, -ki], 1), jnp.concatenate([ki, kr], 1)], 0
    )
    kh, kl = split_table(kernel)
    th, tl = split_table(doppler_table(pulses))
    full = lambda a: pl.BlockSpec(a.shape, lambda c: (0,) * a.ndim, pipeline_mode=pl.Buffered(1))
    return pl.pallas_call(
        functools.partial(spectra_kernel, channels, pulses, tiles, wrap),
        grid=(channels,),
        in_specs=[
            pl.BlockSpec((2, 1, pulses, gates), lambda c: (0, c, 0, 0)),
            pl.BlockSpec((2, 1, pulses, LANES), lambda c: (0, c, 0, 0)),
            full(kh), full(kl), full(th), full(tl),
        ],
        out_specs=pl.BlockSpec((2, tiles, (pulses + wrap) * channels, LANES), lambda c: (0, 0, 0, 0)),
        out_shape=jax.ShapeDtypeStruct((2, tiles, (pulses + wrap) * channels, LANES), F32),
        compiler_params=pltpu.CompilerParams(vmem_limit_bytes=VMEM_LIMIT),
        name="spectra",
    )(echoes, rim, kh, kl, th, tl)


def gram_kernel(bins, channels, tiles, scaling, w_ref, r_ref, f_ref, z_ref, o_ref):
    first = pl.program_id(0) * bins
    order = 2 * channels
    rows = lax.broadcasted_iota(jnp.int32, (order, order), 0)
    cols = lax.broadcasted_iota(jnp.int32, (order, order), 1)
    upper = rows <= cols

    def parts(j, part, t):
        now = r_ref[part, t, j]
        after = r_ref[part, t, j + 1] if j + 1 < bins else f_ref[part, t, 0]
        return jnp.concatenate([now, after], 0)

    for j in range(bins):
        pieces = [[parts(j, part, t) for t in range(tiles)] for part in range(2)]
        whole = jnp.concatenate([jnp.concatenate(p, 1) for p in pieces], 0)
        masked = jnp.concatenate(
            [
                jnp.concatenate(
                    [pieces[part][t] * w_ref[first + j, t] for t in range(tiles)], 1
                )
                for part in range(2)
            ],
            0,
        )
        g = dot3(split(masked), split(whole), ((1,), (1,)))
        re = g[:order, :order] + g[order:, order:]
        im = g[:order, order:] - g[order:, :order]
        z_ref[j] = jnp.where(upper, re, im) * scaling
        for part in range(2):
            for t in range(tiles):
                o_ref[part, j, :, t * LANES : (t + 1) * LANES] = r_ref[part, t, j].astype(BF)


def make_gram(turned, firsts, weights, scaling, bins):
    _, tiles, total, channels, _ = turned.shape
    order = 2 * channels
    return pl.pallas_call(
        functools.partial(gram_kernel, bins, channels, tiles, scaling),
        grid=(total // bins,),
        in_specs=[
            pl.BlockSpec(memory_space=pltpu.SMEM),
            pl.BlockSpec((2, tiles, bins, channels, LANES), lambda i: (0, 0, i, 0, 0)),
            pl.BlockSpec((2, tiles, 1, channels, LANES), lambda i: (0, 0, i, 0, 0)),
        ],
        out_specs=[
            pl.BlockSpec((bins, order, order), lambda i: (i, 0, 0)),
            pl.BlockSpec((2, bins, channels, tiles * LANES), lambda i: (0, i, 0, 0)),
        ],
        out_shape=[
            jax.ShapeDtypeStruct((total, order, order), F32),
            jax.ShapeDtypeStruct((2, total, channels, tiles * LANES), BF),
        ],
        compiler_params=pltpu.CompilerParams(vmem_limit_bytes=VMEM_LIMIT),
        name="gram",
    )(weights, turned, firsts)


def exchange_kernel(
    chunk, scaling, w_ref, s_ref, share_ref, o_ref,
    r_ref, z_ref, got_ref, own_sem, send_sem, recv_sem, zsend_sem, zrecv_sem,
):
    owners, ranges = lax.axis_size("chan"), lax.axis_size("range")
    me, here = lax.axis_index("chan"), lax.axis_index("range")
    _, tiles, _, channels, _ = s_ref.shape
    total = o_ref.shape[1]
    order = share_ref.shape[-1]
    count = total // chunk
    part = chunk // ranges

    def chan_peer(k):
        return {"chan": lax.rem(me + k, owners)}

    def range_peer(k):
        return {"range": lax.rem(here + k, ranges)}

    barrier = pltpu.get_barrier_semaphore()
    for k in range(1, owners):
        pl.semaphore_signal(
            barrier, inc=1, device_id=chan_peer(k), device_id_type=pl.DeviceIdType.MESH
        )
    for k in range(1, ranges):
        pl.semaphore_signal(
            barrier, inc=1, device_id=range_peer(k), device_id_type=pl.DeviceIdType.MESH
        )
    pl.semaphore_wait(barrier, owners + ranges - 2)

    def span(c):
        return (0, chunk + 1) if c == 0 else (c * chunk + 1, chunk)

    mine = pl.ds(pl.multiple_of(me * channels, channels), channels)

    def outgoing(c, k):
        start, size = span(c)
        owner = lax.rem(me + k, owners)
        return pltpu.make_async_remote_copy(
            src_ref=s_ref.at[:, :, pl.ds(owner * total + start, size)],
            dst_ref=r_ref.at[:, :, pl.ds(start, size), mine],
            send_sem=send_sem.at[c, k - 1],
            recv_sem=recv_sem.at[c, k - 1],
            device_id=chan_peer(k),
            device_id_type=pl.DeviceIdType.MESH,
        )

    def local(c):
        start, size = span(c)
        return pltpu.make_async_copy(
            s_ref.at[:, :, pl.ds(me * total + start, size)],
            r_ref.at[:, :, pl.ds(start, size), mine],
            own_sem.at[c],
        )

    def summand(c, k):
        target = lax.rem(here + k, ranges)
        return pltpu.make_async_remote_copy(
            src_ref=z_ref.at[pl.ds(c * chunk + target * part, part)],
            dst_ref=got_ref.at[c, k - 1],
            send_sem=zsend_sem.at[c, k - 1],
            recv_sem=zrecv_sem.at[c, k - 1],
            device_id=range_peer(k),
            device_id_type=pl.DeviceIdType.MESH,
        )

    for c in range(count):
        for k in range(1, owners):
            outgoing(c, k).start()
        local(c).start()

    rows = lax.broadcasted_iota(jnp.int32, (order, order), 0)
    cols = lax.broadcasted_iota(jnp.int32, (order, order), 1)
    upper = rows <= cols

    def collect(c):
        for k in range(1, ranges):
            summand(c, k).wait_recv()

        @pl.loop(0, part)
        def _(j):
            value = z_ref[c * chunk + here * part + j]
            for k in range(1, ranges):
                value = value + got_ref[c, k - 1, j]
            share_ref[c * part + j] = value

    for c in range(count):
        for k in range(1, owners):
            outgoing(c, k).wait_recv()
        local(c).wait()

        @pl.loop(0, chunk)
        def _(i):
            j = c * chunk + i
            pieces = [
                [r_ref[p, t, pl.ds(j, 2)].reshape(order, LANES) for t in range(tiles)]
                for p in range(2)
            ]
            whole = jnp.concatenate([jnp.concatenate(p, 1) for p in pieces], 0)
            masked = jnp.concatenate(
                [
                    jnp.concatenate([pieces[p][t] * w_ref[j, t] for t in range(tiles)], 1)
                    for p in range(2)
                ],
                0,
            )
            g = dot3(split(masked), split(whole), ((1,), (1,)))
            re = g[:order, :order] + g[order:, order:]
            im = g[:order, order:] - g[order:, :order]
            z_ref[j] = jnp.where(upper, re, im) * scaling

        @pl.loop(0, chunk)
        def _(i):
            j = c * chunk + i
            for p in range(2):
                for t in range(tiles):
                    o_ref[p, j, :, t * LANES : (t + 1) * LANES] = r_ref[p, t, j].astype(BF)

        for k in range(1, ranges):
            summand(c, k).start()
        if c > 0:
            collect(c - 1)
    collect(count - 1)
    for c in range(count):
        for k in range(1, owners):
            outgoing(c, k).wait_send()
        for k in range(1, ranges):
            summand(c, k).wait_send()


def exchange(spectra, weights, scaling, chunk, owners, ranges):
    _, tiles, _, channels, _ = spectra.shape
    total = weights.shape[0]
    full = channels * owners
    order = 2 * full
    count = total // chunk
    part = chunk // ranges
    dma = pltpu.SemaphoreType.DMA
    return pl.pallas_call(
        functools.partial(exchange_kernel, chunk, scaling),
        in_specs=[
            pl.BlockSpec(memory_space=pltpu.SMEM),
            pl.BlockSpec(memory_space=pl.ANY),
        ],
        out_specs=[pl.BlockSpec(memory_space=pltpu.VMEM)] * 2,
        out_shape=[
            jax.ShapeDtypeStruct((count * part, order, order), F32),
            jax.ShapeDtypeStruct((2, total, full, tiles * LANES), BF),
        ],
        scratch_shapes=[
            pltpu.VMEM((2, tiles, total + 1, full, LANES), F32),
            pltpu.VMEM((total, order, order), F32),
            pltpu.VMEM((count, ranges - 1, part, order, order), F32),
            dma((count,)),
            dma((count, owners - 1)),
            dma((count, owners - 1)),
            dma((count, ranges - 1)),
            dma((count, ranges - 1)),
        ],
        compiler_params=pltpu.CompilerParams(
            vmem_limit_bytes=VMEM_LIMIT, collective_id=0, has_side_effects=True
        ),
        name="exchange",
    )(weights, spectra)


def factor_kernel(count, order, z_ref, o_ref, re_ref, im_ref, sr_ref, si_ref):
    rows = lax.broadcasted_iota(jnp.int32, (order, order), 0)
    cols = lax.broadcasted_iota(jnp.int32, (order, order), 1)
    lane = lax.broadcasted_iota(jnp.int32, (count, order), 1)

    @pl.loop(0, count)
    def _(b):
        z = z_ref[b]
        re_ref[b] = z
        im_ref[b] = jnp.where(rows < cols, -z.T, 0.0)

    for offset in range(0, order, STRIP):
        for b in range(count):
            sr_ref[pl.ds(b, STRIP, stride=count), :] = re_ref[b, offset : offset + STRIP, :]
            si_ref[pl.ds(b, STRIP, stride=count), :] = im_ref[b, offset : offset + STRIP, :]
        now_r = [sr_ref[i * count : (i + 1) * count, :] for i in range(STRIP)]
        now_i = [si_ref[i * count : (i + 1) * count, :] for i in range(STRIP)]
        for i in range(STRIP):
            k = offset + i
            pivot = jnp.broadcast_to(now_r[i][:, k : k + 1], (count, order))
            root = lax.rsqrt(pivot)
            row_r = jnp.where(lane >= k, now_r[i] * root, 0.0)
            row_i = jnp.where(lane > k, now_i[i] * root, 0.0)
            for j in range(i + 1, STRIP):
                m = offset + j
                cr = jnp.broadcast_to(row_r[:, m : m + 1], (count, order))
                ci = jnp.broadcast_to(row_i[:, m : m + 1], (count, order))
                now_r[j] = now_r[j] - cr * row_r - ci * row_i
                now_i[j] = now_i[j] - cr * row_i + ci * row_r
            sr_ref[i * count : (i + 1) * count, :] = row_r
            si_ref[i * count : (i + 1) * count, :] = row_i
        done = offset + STRIP

        for b in range(count):
            fr = sr_ref[pl.ds(b, STRIP, stride=count), :]
            fi = si_ref[pl.ds(b, STRIP, stride=count), :]
            o_ref[b, 0, offset:done, :] = fr
            o_ref[b, 1, offset:done, :] = fi
            if done < order:
                left = jnp.concatenate([fr, fi], 0)
                right = jnp.concatenate(
                    [jnp.concatenate([fr, fi], 0), jnp.concatenate([fi, -fr], 0)], 1
                )
                lh, ll = split(left)
                rh, rl = split(right)
                update = dot(
                    jnp.concatenate([lh, lh, ll], 0)[:, :],
                    jnp.concatenate([rh, rl, rh], 0),
                    ((0,), (0,)),
                )
                re_ref[b, done:, :] = re_ref[b, done:, :] - update[done:, :order]
                im_ref[b, done:, :] = im_ref[b, done:, :] - update[done:, order:]


def make_factor(gram):
    count, order, _ = gram.shape
    return pl.pallas_call(
        functools.partial(factor_kernel, count, order),
        out_shape=jax.ShapeDtypeStruct((count, 2, order, order), F32),
        scratch_shapes=[
            pltpu.VMEM((count, order, order), F32),
            pltpu.VMEM((count, order, order), F32),
            pltpu.VMEM((STRIP * count, order), F32),
            pltpu.VMEM((STRIP * count, order), F32),
        ],
        compiler_params=pltpu.CompilerParams(vmem_limit_bytes=VMEM_LIMIT),
        name="factor",
    )(gram)


def pack_factor(factors):
    order = factors.shape[-1]
    keep = jnp.arange(order)[:, None] <= jnp.arange(order)[None, :]
    return jnp.where(keep, factors[:, 0], jnp.swapaxes(factors[:, 1], 1, 2))


def unpack_kernel(p_ref, o_ref):
    order = p_ref.shape[-1]
    rows = lax.broadcasted_iota(jnp.int32, (order, order), 0)
    cols = lax.broadcasted_iota(jnp.int32, (order, order), 1)
    for b in range(p_ref.shape[0]):
        z = p_ref[b]
        o_ref[b, 0] = jnp.where(rows <= cols, z, 0.0)
        o_ref[b, 1] = jnp.where(rows < cols, z.T, 0.0)


def unpack_factor(packed, count):
    ranges, share, order, _ = packed.shape
    bins = share // count
    packed = packed.reshape(ranges, count, bins, order, order)
    return pl.pallas_call(
        unpack_kernel,
        grid=(count, ranges),
        in_specs=[
            pl.BlockSpec((None, None, bins, order, order), lambda c, r: (r, c, 0, 0, 0))
        ],
        out_specs=pl.BlockSpec(
            (bins, 2, order, order), lambda c, r: (c * ranges + r, 0, 0, 0)
        ),
        out_shape=jax.ShapeDtypeStruct((ranges * share, 2, order, order), F32),
        name="unpack",
    )(packed)


def on_device(echoes, chirp, train_mask):
    tap_span = chirp.shape[-1] - 1
    _, channels, pulses, gates = echoes.shape
    tiles = gates // LANES
    ranges, owners = lax.axis_size("range"), lax.axis_size("chan")
    total = train_mask.shape[0]
    chunk = total // CHUNKS
    rim = from_behind(echoes[..., :tap_span], "range", -1)
    weights = train_mask.astype(F32)
    scaling = 1.0 / (gates * ranges)
    wrap = int(channels % 8 == 0 and chunk % ranges == 0)
    spectra = make_spectra(echoes, rim, chirp, wrap)
    spectra = spectra.reshape(2, tiles, pulses + wrap, channels, LANES)
    if wrap:
        count = CHUNKS
        share, spectra_out = exchange(spectra, weights, scaling, chunk, owners, ranges)
    else:
        count = 1
        turned = lax.all_to_all(spectra, "chan", split_axis=2, concat_axis=3, tiled=True)
        edge = from_behind_2(turned[:, :, :1], "chan", -1)
        bins = math.gcd(total, 8)
        firsts = jnp.concatenate([turned[:, :, bins::bins], edge], 2)
        packed, spectra_out = make_gram(turned, firsts, weights, scaling, bins)
        share = lax.psum_scatter(packed, "range", scatter_dimension=0, tiled=True)
    mine = pack_factor(make_factor(share))
    factors = unpack_factor(lax.all_gather(mine, "range", axis=0), count)
    return (spectra_out, factors)


def solution(mesh):
    return jax.shard_map(
        on_device,
        mesh=mesh,
        in_specs=(P(None, "chan", None, "range"), P(), P("chan", "range")),
        out_specs=(P(None, "chan", None, "range"), P("chan", None, None, None)),
        check_vma=False,
    )
```

```python
import functools
import math

import jax
import jax.numpy as jnp
from jax import lax
from jax.experimental import pallas as pl
from jax.experimental.pallas import tpu as pltpu
from jax.sharding import PartitionSpec as P

LANES = 128
STRIP = 16
CHUNKS = 4
BF = jnp.bfloat16
F32 = jnp.float32
VMEM_LIMIT = 60 * 1024 * 1024


def split(x):
    high = x.astype(BF)
    return high, (x - high.astype(F32)).astype(BF)


def split_table(x):
    high = lax.reduce_precision(x, 8, 7)
    return high.astype(BF), (x - high).astype(BF)


def dot(a, b, dims=((1,), (0,))):
    return lax.dot_general(a, b, (dims, ((), ())), preferred_element_type=F32)


def dot3(a, b, dims=((1,), (0,))):
    (ah, al), (bh, bl) = a, b
    return dot(ah, bh, dims) + (dot(ah, bl, dims) + dot(al, bh, dims))


def from_behind(value, axis, steps):
    count = lax.axis_size(axis)
    leading, last = (max(0, -steps), min(count, count - steps))
    return lax.ppermute(value, axis, [(s, s + steps) for s in range(leading, last)])


def from_behind_2(block, axis, distance):
    devices = range(lax.axis_size(axis))
    route = [((i - distance) % len(devices), i) for i in devices]
    return lax.ppermute(block, axis, route)


def toeplitz_rows(taps):
    tap_span = taps.shape[-1] - 1
    padded = jnp.concatenate([taps, jnp.zeros((taps.shape[0], tap_span), taps.dtype)], -1)
    tiled = jnp.tile(padded, (1, tap_span))
    return tiled[:, : 2 * tap_span * tap_span].reshape(taps.shape[0], tap_span, 2 * tap_span)


def doppler_table(pulses):
    half = jnp.arange(pulses // 2, dtype=jnp.int32)
    bins = jnp.concatenate([2 * half, 2 * half + 1])
    phase = bins[:, None] * half[None, :] % pulses
    angles = phase.astype(F32) * (2.0 * math.pi / pulses)
    scaling = 1.0 / math.sqrt(pulses)
    return jnp.concatenate([jnp.cos(angles) * scaling, -jnp.sin(angles) * scaling])


def spectra_kernel(channels, pulses, tiles, wrap, e_ref, h_ref, kh_ref, kl_ref, th_ref, tl_ref, s_ref):
    channel = pl.program_id(0)
    kernel = (kh_ref[...], kl_ref[...])
    wide = [jnp.concatenate([e_ref[p, 0], h_ref[p, 0]], -1) for p in range(2)]
    for t in range(tiles):
        window = jnp.concatenate(
            [w[:, t * LANES : (t + 2) * LANES] for w in wide], -1
        )
        y = dot3(split(window), kernel)
        half = pulses // 2
        folded = (split(y[:half] + y[half:]), split(y[:half] - y[half:]))
        for b in range(2):
            top, low = pl.ds(b * half, half), pl.ds((2 + b) * half, half)
            re = dot3((th_ref[top, :], tl_ref[top, :]), folded[b])
            im = dot3((th_ref[low, :], tl_ref[low, :]), folded[b])
            rows = pl.ds(b * channels + channel, half, stride=2 * channels)
            real = re[:, :LANES] - im[:, LANES:]
            imag = re[:, LANES:] + im[:, :LANES]
            s_ref[0, t, rows, :] = real
            s_ref[1, t, rows, :] = imag
            if wrap and b == 0:
                s_ref[0, t, pl.ds(pulses * channels + channel, 1), :] = real[:1]
                s_ref[1, t, pl.ds(pulses * channels + channel, 1), :] = imag[:1]


def make_spectra(echoes, rim, chirp, wrap):
    _, channels, pulses, gates = echoes.shape
    tiles = gates // LANES
    rows = toeplitz_rows(chirp)
    kr, ki = rows[0].T, rows[1].T
    kernel = jnp.concatenate(
        [jnp.concatenate([kr, -ki], 1), jnp.concatenate([ki, kr], 1)], 0
    )
    kh, kl = split_table(kernel)
    th, tl = split_table(doppler_table(pulses))
    full = lambda a: pl.BlockSpec(a.shape, lambda c: (0,) * a.ndim, pipeline_mode=pl.Buffered(1))
    return pl.pallas_call(
        functools.partial(spectra_kernel, channels, pulses, tiles, wrap),
        grid=(channels,),
        in_specs=[
            pl.BlockSpec((2, 1, pulses, gates), lambda c: (0, c, 0, 0)),
            pl.BlockSpec((2, 1, pulses, LANES), lambda c: (0, c, 0, 0)),
            full(kh), full(kl), full(th), full(tl),
        ],
        out_specs=pl.BlockSpec((2, tiles, (pulses + wrap) * channels, LANES), lambda c: (0, 0, 0, 0)),
        out_shape=jax.ShapeDtypeStruct((2, tiles, (pulses + wrap) * channels, LANES), F32),
        compiler_params=pltpu.CompilerParams(vmem_limit_bytes=VMEM_LIMIT),
        name="spectra",
    )(echoes, rim, kh, kl, th, tl)


def gram_kernel(bins, channels, tiles, scaling, w_ref, r_ref, f_ref, z_ref, o_ref):
    first = pl.program_id(0) * bins
    order = 2 * channels
    rows = lax.broadcasted_iota(jnp.int32, (order, order), 0)
    cols = lax.broadcasted_iota(jnp.int32, (order, order), 1)
    upper = rows <= cols

    def parts(j, part, t):
        now = r_ref[part, t, j]
        after = r_ref[part, t, j + 1] if j + 1 < bins else f_ref[part, t, 0]
        return jnp.concatenate([now, after], 0)

    for j in range(bins):
        pieces = [[parts(j, part, t) for t in range(tiles)] for part in range(2)]
        whole = jnp.concatenate([jnp.concatenate(p, 1) for p in pieces], 0)
        masked = jnp.concatenate(
            [
                jnp.concatenate(
                    [pieces[part][t] * w_ref[first + j, t] for t in range(tiles)], 1
                )
                for part in range(2)
            ],
            0,
        )
        g = dot3(split(masked), split(whole), ((1,), (1,)))
        re = g[:order, :order] + g[order:, order:]
        im = g[:order, order:] - g[order:, :order]
        z_ref[j] = jnp.where(upper, re, im) * scaling
        for part in range(2):
            for t in range(tiles):
                o_ref[part, j, :, t * LANES : (t + 1) * LANES] = r_ref[part, t, j].astype(BF)


def make_gram(turned, firsts, weights, scaling, bins):
    _, tiles, total, channels, _ = turned.shape
    order = 2 * channels
    return pl.pallas_call(
        functools.partial(gram_kernel, bins, channels, tiles, scaling),
        grid=(total // bins,),
        in_specs=[
            pl.BlockSpec(memory_space=pltpu.SMEM),
            pl.BlockSpec((2, tiles, bins, channels, LANES), lambda i: (0, 0, i, 0, 0)),
            pl.BlockSpec((2, tiles, 1, channels, LANES), lambda i: (0, 0, i, 0, 0)),
        ],
        out_specs=[
            pl.BlockSpec((bins, order, order), lambda i: (i, 0, 0)),
            pl.BlockSpec((2, bins, channels, tiles * LANES), lambda i: (0, i, 0, 0)),
        ],
        out_shape=[
            jax.ShapeDtypeStruct((total, order, order), F32),
            jax.ShapeDtypeStruct((2, total, channels, tiles * LANES), BF),
        ],
        compiler_params=pltpu.CompilerParams(vmem_limit_bytes=VMEM_LIMIT),
        name="gram",
    )(weights, turned, firsts)


def exchange_kernel(
    chunk, scaling, w_ref, s_ref, share_ref, o_ref,
    r_ref, z_ref, got_ref, t_ref, own_sem, send_sem, recv_sem, zsend_sem, zrecv_sem,
):
    owners, ranges = lax.axis_size("chan"), lax.axis_size("range")
    me, here = lax.axis_index("chan"), lax.axis_index("range")
    _, tiles, _, channels, _ = s_ref.shape
    total = o_ref.shape[1]
    order = share_ref.shape[-1]
    count = total // chunk
    part = chunk // ranges

    side = lax.rem(here, 2)

    def target(k):
        return lax.rem(me + k + side * (owners - 2 * k), owners)

    def chan_peer(k):
        return {"chan": target(k)}

    def range_peer(k):
        return {"range": lax.rem(here + k, ranges)}

    barrier = pltpu.get_barrier_semaphore()
    for k in range(1, owners):
        pl.semaphore_signal(
            barrier, inc=1, device_id=chan_peer(k), device_id_type=pl.DeviceIdType.MESH
        )
    for k in range(1, ranges):
        pl.semaphore_signal(
            barrier, inc=1, device_id=range_peer(k), device_id_type=pl.DeviceIdType.MESH
        )
    pl.semaphore_wait(barrier, owners + ranges - 2)

    def span(c):
        return (0, chunk + 1) if c == 0 else (c * chunk + 1, chunk)

    mine = pl.ds(pl.multiple_of(me * channels, channels), channels)

    def outgoing(c, k):
        start, size = span(c)
        owner = target(k)
        return pltpu.make_async_remote_copy(
            src_ref=s_ref.at[:, :, pl.ds(owner * total + start, size)],
            dst_ref=r_ref.at[:, :, pl.ds(start, size), mine],
            send_sem=send_sem.at[c, k - 1],
            recv_sem=recv_sem.at[c, k - 1],
            device_id=chan_peer(k),
            device_id_type=pl.DeviceIdType.MESH,
        )

    def local(c):
        start, size = span(c)
        return pltpu.make_async_copy(
            s_ref.at[:, :, pl.ds(me * total + start, size)],
            r_ref.at[:, :, pl.ds(start, size), mine],
            own_sem.at[c],
        )

    twin = here + 1 - 2 * lax.rem(here, 2)
    over = lax.rem(here + 2, ranges)
    far = lax.rem(twin + 2, ranges)

    def summand(c, k):
        source = z_ref.at[pl.ds(c * chunk + (twin, far)[k] * part, part)] if k < 2 else t_ref.at[c]
        return pltpu.make_async_remote_copy(
            src_ref=source,
            dst_ref=got_ref.at[c, k],
            send_sem=zsend_sem.at[c, k],
            recv_sem=zrecv_sem.at[c, k],
            device_id={"range": twin if k < 2 else over},
            device_id_type=pl.DeviceIdType.MESH,
        )

    for c in range(count):
        for k in range(1, owners):
            outgoing(c, k).start()
        local(c).start()

    rows = lax.broadcasted_iota(jnp.int32, (order, order), 0)
    cols = lax.broadcasted_iota(jnp.int32, (order, order), 1)
    upper = rows <= cols

    def relay(c):
        summand(c, 1).wait_recv()
        t_ref[c] = z_ref[pl.ds(c * chunk + over * part, part)] + got_ref[c, 1]
        summand(c, 0).wait_recv()
        share_ref[pl.ds(c * part, part)] = (
            z_ref[pl.ds(c * chunk + here * part, part)] + got_ref[c, 0]
        )
        summand(c, 2).start()

    def collect(c):
        summand(c, 2).wait_recv()
        span = pl.ds(c * part, part)
        share_ref[span] = share_ref[span] + got_ref[c, 2]

    for c in range(count):
        for k in range(1, owners):
            outgoing(c, k).wait_recv()
        local(c).wait()

        @pl.loop(0, chunk)
        def _(i):
            j = c * chunk + i
            pieces = [
                [r_ref[p, t, pl.ds(j, 2)].reshape(order, LANES) for t in range(tiles)]
                for p in range(2)
            ]
            whole = jnp.concatenate([jnp.concatenate(p, 1) for p in pieces], 0)
            masked = jnp.concatenate(
                [
                    jnp.concatenate([pieces[p][t] * w_ref[j, t] for t in range(tiles)], 1)
                    for p in range(2)
                ],
                0,
            )
            g = dot3(split(masked), split(whole), ((1,), (1,)))
            re = g[:order, :order] + g[order:, order:]
            im = g[:order, order:] - g[order:, :order]
            z_ref[j] = jnp.where(upper, re, im) * scaling

        @pl.loop(0, chunk)
        def _(i):
            j = c * chunk + i
            for p in range(2):
                for t in range(tiles):
                    o_ref[p, j, :, t * LANES : (t + 1) * LANES] = r_ref[p, t, j].astype(BF)

        for k in range(2):
            summand(c, 1 - k).start()
        if c > 0:
            relay(c - 1)
        if c > 1:
            collect(c - 2)
    relay(count - 1)
    for c in range(max(0, count - 2), count):
        collect(c)
    for c in range(count):
        for k in range(1, owners):
            outgoing(c, k).wait_send()
        for k in range(3):
            summand(c, k).wait_send()


def exchange(spectra, weights, scaling, chunk, owners, ranges):
    _, tiles, _, channels, _ = spectra.shape
    total = weights.shape[0]
    full = channels * owners
    order = 2 * full
    count = total // chunk
    part = chunk // ranges
    dma = pltpu.SemaphoreType.DMA
    return pl.pallas_call(
        functools.partial(exchange_kernel, chunk, scaling),
        in_specs=[
            pl.BlockSpec(memory_space=pltpu.SMEM),
            pl.BlockSpec(memory_space=pl.ANY),
        ],
        out_specs=[pl.BlockSpec(memory_space=pltpu.VMEM)] * 2,
        out_shape=[
            jax.ShapeDtypeStruct((count * part, order, order), F32),
            jax.ShapeDtypeStruct((2, total, full, tiles * LANES), BF),
        ],
        scratch_shapes=[
            pltpu.VMEM((2, tiles, total + 1, full, LANES), F32),
            pltpu.VMEM((total, order, order), F32),
            pltpu.VMEM((count, 3, part, order, order), F32),
            pltpu.VMEM((count, part, order, order), F32),
            dma((count,)),
            dma((count, owners - 1)),
            dma((count, owners - 1)),
            dma((count, 3)),
            dma((count, 3)),
        ],
        compiler_params=pltpu.CompilerParams(
            vmem_limit_bytes=VMEM_LIMIT, collective_id=0, has_side_effects=True
        ),
        name="exchange",
    )(weights, spectra)


def factor_kernel(count, order, z_ref, o_ref, re_ref, im_ref, sr_ref, si_ref):
    rows = lax.broadcasted_iota(jnp.int32, (order, order), 0)
    cols = lax.broadcasted_iota(jnp.int32, (order, order), 1)
    lane = lax.broadcasted_iota(jnp.int32, (count, order), 1)

    @pl.loop(0, count)
    def _(b):
        z = z_ref[b]
        re_ref[b] = z
        im_ref[b] = jnp.where(rows < cols, -z.T, 0.0)

    for offset in range(0, order, STRIP):
        for b in range(count):
            sr_ref[pl.ds(b, STRIP, stride=count), :] = re_ref[b, offset : offset + STRIP, :]
            si_ref[pl.ds(b, STRIP, stride=count), :] = im_ref[b, offset : offset + STRIP, :]
        now_r = [sr_ref[i * count : (i + 1) * count, :] for i in range(STRIP)]
        now_i = [si_ref[i * count : (i + 1) * count, :] for i in range(STRIP)]
        for i in range(STRIP):
            k = offset + i
            pivot = jnp.broadcast_to(now_r[i][:, k : k + 1], (count, order))
            root = lax.rsqrt(pivot)
            row_r = jnp.where(lane >= k, now_r[i] * root, 0.0)
            row_i = jnp.where(lane > k, now_i[i] * root, 0.0)
            for j in range(i + 1, STRIP):
                m = offset + j
                cr = jnp.broadcast_to(row_r[:, m : m + 1], (count, order))
                ci = jnp.broadcast_to(row_i[:, m : m + 1], (count, order))
                now_r[j] = now_r[j] - cr * row_r - ci * row_i
                now_i[j] = now_i[j] - cr * row_i + ci * row_r
            sr_ref[i * count : (i + 1) * count, :] = row_r
            si_ref[i * count : (i + 1) * count, :] = row_i
        done = offset + STRIP

        for b in range(count):
            fr = sr_ref[pl.ds(b, STRIP, stride=count), :]
            fi = si_ref[pl.ds(b, STRIP, stride=count), :]
            re_ref[b, offset:done, :] = fr
            im_ref[b, offset:done, :] = fi
            if done < order:
                left = jnp.concatenate([fr, fi], 0)
                right = jnp.concatenate(
                    [jnp.concatenate([fr, fi], 0), jnp.concatenate([fi, -fr], 0)], 1
                )
                lh, ll = split(left)
                rh, rl = split(right)
                update = dot(
                    jnp.concatenate([lh, lh, ll], 0)[:, :],
                    jnp.concatenate([rh, rl, rh], 0),
                    ((0,), (0,)),
                )
                re_ref[b, done:, :] = re_ref[b, done:, :] - update[done:, :order]
                im_ref[b, done:, :] = im_ref[b, done:, :] - update[done:, order:]

    @pl.loop(0, count)
    def _(b):
        o_ref[b] = jnp.where(rows <= cols, re_ref[b], im_ref[b].T)


def make_factor(gram):
    count, order, _ = gram.shape
    return pl.pallas_call(
        functools.partial(factor_kernel, count, order),
        out_shape=jax.ShapeDtypeStruct((count, order, order), F32),
        scratch_shapes=[
            pltpu.VMEM((count, order, order), F32),
            pltpu.VMEM((count, order, order), F32),
            pltpu.VMEM((STRIP * count, order), F32),
            pltpu.VMEM((STRIP * count, order), F32),
        ],
        compiler_params=pltpu.CompilerParams(vmem_limit_bytes=VMEM_LIMIT),
        name="factor",
    )(gram)


def gather_kernel(pieces, p_ref, o_ref, own_sem, send_sem, recv_sem):
    here = lax.axis_index("range")
    twin = here + 1 - 2 * lax.rem(here, 2)
    over = lax.rem(here + 2, 4)
    size = p_ref.shape[0] // pieces

    barrier = pltpu.get_barrier_semaphore()
    for peer in (twin, over):
        pl.semaphore_signal(
            barrier, inc=1, device_id={"range": peer}, device_id_type=pl.DeviceIdType.MESH
        )
    pl.semaphore_wait(barrier, 2)

    def send(kind, q):
        span = pl.ds(q * size, size)
        owner, peer = ((here, over), (here, twin), (over, twin))[kind]
        return pltpu.make_async_remote_copy(
            src_ref=p_ref.at[span] if kind < 2 else o_ref.at[owner, span],
            dst_ref=o_ref.at[owner, span],
            send_sem=send_sem.at[kind, q],
            recv_sem=recv_sem.at[kind, q],
            device_id={"range": peer},
            device_id_type=pl.DeviceIdType.MESH,
        )

    for kind in range(2):
        for q in range(pieces):
            send(kind, q).start()
    own = pltpu.make_async_copy(p_ref, o_ref.at[here], own_sem)
    own.start()
    for q in range(pieces):
        send(0, q).wait_recv()
        send(2, q).start()
    for q in range(pieces):
        send(1, q).wait_recv()
        send(2, q).wait_recv()
        for kind in range(3):
            send(kind, q).wait_send()
    own.wait()


def gather(packed):
    pieces = math.gcd(packed.shape[0], 4)
    dma = pltpu.SemaphoreType.DMA
    return pl.pallas_call(
        functools.partial(gather_kernel, pieces),
        in_specs=[pl.BlockSpec(memory_space=pltpu.VMEM)],
        out_specs=pl.BlockSpec(memory_space=pl.ANY),
        out_shape=jax.ShapeDtypeStruct((4,) + packed.shape, F32),
        scratch_shapes=[dma, dma((3, pieces)), dma((3, pieces))],
        compiler_params=pltpu.CompilerParams(collective_id=1, has_side_effects=True),
        name="gather",
    )(packed)


def unpack_kernel(p_ref, o_ref):
    order = p_ref.shape[-1]
    rows = lax.broadcasted_iota(jnp.int32, (order, order), 0)
    cols = lax.broadcasted_iota(jnp.int32, (order, order), 1)
    for b in range(p_ref.shape[0]):
        z = p_ref[b]
        o_ref[b, 0] = jnp.where(rows <= cols, z, 0.0)
        o_ref[b, 1] = jnp.where(rows < cols, z.T, 0.0)


def unpack_factor(packed, count):
    ranges, share, order, _ = packed.shape
    bins = share // count
    packed = packed.reshape(ranges, count, bins, order, order)
    return pl.pallas_call(
        unpack_kernel,
        grid=(count, ranges),
        in_specs=[
            pl.BlockSpec((None, None, bins, order, order), lambda c, r: (r, c, 0, 0, 0))
        ],
        out_specs=pl.BlockSpec(
            (bins, 2, order, order), lambda c, r: (c * ranges + r, 0, 0, 0)
        ),
        out_shape=jax.ShapeDtypeStruct((ranges * share, 2, order, order), F32),
        name="unpack",
    )(packed)


def on_device(echoes, chirp, train_mask):
    tap_span = chirp.shape[-1] - 1
    _, channels, pulses, gates = echoes.shape
    tiles = gates // LANES
    ranges, owners = lax.axis_size("range"), lax.axis_size("chan")
    total = train_mask.shape[0]
    chunk = total // CHUNKS
    rim = from_behind(echoes[..., :tap_span], "range", -1)
    weights = train_mask.astype(F32)
    scaling = 1.0 / (gates * ranges)
    wrap = int(channels % 8 == 0 and chunk % ranges == 0 and ranges == 4)
    spectra = make_spectra(echoes, rim, chirp, wrap)
    spectra = spectra.reshape(2, tiles, pulses + wrap, channels, LANES)
    if wrap:
        count = CHUNKS
        share, spectra_out = exchange(spectra, weights, scaling, chunk, owners, ranges)
    else:
        count = 1
        turned = lax.all_to_all(spectra, "chan", split_axis=2, concat_axis=3, tiled=True)
        edge = from_behind_2(turned[:, :, :1], "chan", -1)
        bins = math.gcd(total, 8)
        firsts = jnp.concatenate([turned[:, :, bins::bins], edge], 2)
        packed, spectra_out = make_gram(turned, firsts, weights, scaling, bins)
        share = lax.psum_scatter(packed, "range", scatter_dimension=0, tiled=True)
    mine = make_factor(share)
    pooled = gather(mine) if ranges == 4 else lax.all_gather(mine, "range", axis=0)
    factors = unpack_factor(pooled, count)
    return (spectra_out, factors)


def solution(mesh):
    return jax.shard_map(
        on_device,
        mesh=mesh,
        in_specs=(P(None, "chan", None, "range"), P(), P("chan", "range")),
        out_specs=(P(None, "chan", None, "range"), P("chan", None, None, None)),
        check_vma=False,
    )
```

```python
import functools
import math

import jax
import jax.numpy as jnp
from jax import lax
from jax.experimental import pallas as pl
from jax.experimental.pallas import tpu as pltpu
from jax.sharding import PartitionSpec as P

LANES = 128
STRIP = 16
CHUNKS = 4
BF = jnp.bfloat16
F32 = jnp.float32
VMEM_LIMIT = 60 * 1024 * 1024


def split(x):
    high = x.astype(BF)
    return high, (x - high.astype(F32)).astype(BF)


def split_table(x):
    high = lax.reduce_precision(x, 8, 7)
    return high.astype(BF), (x - high).astype(BF)


def dot(a, b, dims=((1,), (0,))):
    return lax.dot_general(a, b, (dims, ((), ())), preferred_element_type=F32)


def dot3(a, b, dims=((1,), (0,))):
    (ah, al), (bh, bl) = a, b
    return dot(ah, bh, dims) + (dot(ah, bl, dims) + dot(al, bh, dims))


def from_behind(value, axis, steps):
    count = lax.axis_size(axis)
    leading, last = (max(0, -steps), min(count, count - steps))
    return lax.ppermute(value, axis, [(s, s + steps) for s in range(leading, last)])


def from_behind_2(block, axis, distance):
    devices = range(lax.axis_size(axis))
    route = [((i - distance) % len(devices), i) for i in devices]
    return lax.ppermute(block, axis, route)


def toeplitz_rows(taps):
    tap_span = taps.shape[-1] - 1
    padded = jnp.concatenate([taps, jnp.zeros((taps.shape[0], tap_span), taps.dtype)], -1)
    tiled = jnp.tile(padded, (1, tap_span))
    return tiled[:, : 2 * tap_span * tap_span].reshape(taps.shape[0], tap_span, 2 * tap_span)


def doppler_table(pulses):
    half = jnp.arange(pulses // 2, dtype=jnp.int32)
    bins = jnp.concatenate([2 * half, 2 * half + 1])
    phase = bins[:, None] * half[None, :] % pulses
    angles = phase.astype(F32) * (2.0 * math.pi / pulses)
    scaling = 1.0 / math.sqrt(pulses)
    return jnp.concatenate([jnp.cos(angles) * scaling, -jnp.sin(angles) * scaling])


def spectra_kernel(channels, pulses, tiles, wrap, e_ref, h_ref, kh_ref, kl_ref, th_ref, tl_ref, s_ref):
    channel = pl.program_id(0)
    kernel = (kh_ref[...], kl_ref[...])
    wide = [jnp.concatenate([e_ref[p, 0], h_ref[p, 0]], -1) for p in range(2)]
    for t in range(tiles):
        window = jnp.concatenate(
            [w[:, t * LANES : (t + 2) * LANES] for w in wide], -1
        )
        y = dot3(split(window), kernel)
        half = pulses // 2
        folded = (split(y[:half] + y[half:]), split(y[:half] - y[half:]))
        for b in range(2):
            top, low = pl.ds(b * half, half), pl.ds((2 + b) * half, half)
            re = dot3((th_ref[top, :], tl_ref[top, :]), folded[b])
            im = dot3((th_ref[low, :], tl_ref[low, :]), folded[b])
            rows = pl.ds(b * channels + channel, half, stride=2 * channels)
            real = re[:, :LANES] - im[:, LANES:]
            imag = re[:, LANES:] + im[:, :LANES]
            s_ref[0, t, rows, :] = real
            s_ref[1, t, rows, :] = imag
            if wrap and b == 0:
                s_ref[0, t, pl.ds(pulses * channels + channel, 1), :] = real[:1]
                s_ref[1, t, pl.ds(pulses * channels + channel, 1), :] = imag[:1]


def make_spectra(echoes, rim, chirp, wrap):
    _, channels, pulses, gates = echoes.shape
    tiles = gates // LANES
    rows = toeplitz_rows(chirp)
    kr, ki = rows[0].T, rows[1].T
    kernel = jnp.concatenate(
        [jnp.concatenate([kr, -ki], 1), jnp.concatenate([ki, kr], 1)], 0
    )
    kh, kl = split_table(kernel)
    th, tl = split_table(doppler_table(pulses))
    full = lambda a: pl.BlockSpec(a.shape, lambda c: (0,) * a.ndim, pipeline_mode=pl.Buffered(1))
    return pl.pallas_call(
        functools.partial(spectra_kernel, channels, pulses, tiles, wrap),
        grid=(channels,),
        in_specs=[
            pl.BlockSpec((2, 1, pulses, gates), lambda c: (0, c, 0, 0)),
            pl.BlockSpec((2, 1, pulses, LANES), lambda c: (0, c, 0, 0)),
            full(kh), full(kl), full(th), full(tl),
        ],
        out_specs=pl.BlockSpec((2, tiles, (pulses + wrap) * channels, LANES), lambda c: (0, 0, 0, 0)),
        out_shape=jax.ShapeDtypeStruct((2, tiles, (pulses + wrap) * channels, LANES), F32),
        compiler_params=pltpu.CompilerParams(vmem_limit_bytes=VMEM_LIMIT),
        name="spectra",
    )(echoes, rim, kh, kl, th, tl)


def gram_kernel(bins, channels, tiles, scaling, w_ref, r_ref, f_ref, z_ref, o_ref):
    first = pl.program_id(0) * bins
    order = 2 * channels
    rows = lax.broadcasted_iota(jnp.int32, (order, order), 0)
    cols = lax.broadcasted_iota(jnp.int32, (order, order), 1)
    upper = rows <= cols

    def parts(j, part, t):
        now = r_ref[part, t, j]
        after = r_ref[part, t, j + 1] if j + 1 < bins else f_ref[part, t, 0]
        return jnp.concatenate([now, after], 0)

    for j in range(bins):
        pieces = [[parts(j, part, t) for t in range(tiles)] for part in range(2)]
        whole = jnp.concatenate([jnp.concatenate(p, 1) for p in pieces], 0)
        masked = jnp.concatenate(
            [
                jnp.concatenate(
                    [pieces[part][t] * w_ref[first + j, t] for t in range(tiles)], 1
                )
                for part in range(2)
            ],
            0,
        )
        g = dot3(split(masked), split(whole), ((1,), (1,)))
        re = g[:order, :order] + g[order:, order:]
        im = g[:order, order:] - g[order:, :order]
        z_ref[j] = jnp.where(upper, re, im) * scaling
        for part in range(2):
            for t in range(tiles):
                o_ref[part, j, :, t * LANES : (t + 1) * LANES] = r_ref[part, t, j].astype(BF)


def make_gram(turned, firsts, weights, scaling, bins):
    _, tiles, total, channels, _ = turned.shape
    order = 2 * channels
    return pl.pallas_call(
        functools.partial(gram_kernel, bins, channels, tiles, scaling),
        grid=(total // bins,),
        in_specs=[
            pl.BlockSpec(memory_space=pltpu.SMEM),
            pl.BlockSpec((2, tiles, bins, channels, LANES), lambda i: (0, 0, i, 0, 0)),
            pl.BlockSpec((2, tiles, 1, channels, LANES), lambda i: (0, 0, i, 0, 0)),
        ],
        out_specs=[
            pl.BlockSpec((bins, order, order), lambda i: (i, 0, 0)),
            pl.BlockSpec((2, bins, channels, tiles * LANES), lambda i: (0, i, 0, 0)),
        ],
        out_shape=[
            jax.ShapeDtypeStruct((total, order, order), F32),
            jax.ShapeDtypeStruct((2, total, channels, tiles * LANES), BF),
        ],
        compiler_params=pltpu.CompilerParams(vmem_limit_bytes=VMEM_LIMIT),
        name="gram",
    )(weights, turned, firsts)


def exchange_kernel(
    chunk, scaling, w_ref, s_ref, share_ref, o_ref,
    r_ref, z_ref, got_ref, t_ref, own_sem, send_sem, recv_sem, zsend_sem, zrecv_sem,
):
    owners, ranges = lax.axis_size("chan"), lax.axis_size("range")
    me, here = lax.axis_index("chan"), lax.axis_index("range")
    _, tiles, _, channels, _ = s_ref.shape
    total = o_ref.shape[1]
    order = share_ref.shape[-1]
    count = total // chunk
    part = chunk // ranges

    group = owners // 2
    half, place = me // group, lax.rem(me, group)

    def target(k):
        if k < group:
            return half * group + lax.rem(place + k, group)
        return (1 - half) * group + lax.rem(place + k, group)

    def chan_peer(k):
        return {"chan": target(k)}

    def range_peer(k):
        return {"range": lax.rem(here + k, ranges)}

    barrier = pltpu.get_barrier_semaphore()
    for k in range(1, owners):
        pl.semaphore_signal(
            barrier, inc=1, device_id=chan_peer(k), device_id_type=pl.DeviceIdType.MESH
        )
    for k in range(1, ranges):
        pl.semaphore_signal(
            barrier, inc=1, device_id=range_peer(k), device_id_type=pl.DeviceIdType.MESH
        )
    pl.semaphore_wait(barrier, owners + ranges - 2)

    def span(c):
        return (0, chunk + 1) if c == 0 else (c * chunk + 1, chunk)

    mine = pl.ds(pl.multiple_of(me * channels, channels), channels)

    def outgoing(c, k):
        start, size = span(c)
        owner = target(k)
        return pltpu.make_async_remote_copy(
            src_ref=s_ref.at[:, :, pl.ds(owner * total + start, size)],
            dst_ref=r_ref.at[:, :, pl.ds(start, size), mine],
            send_sem=send_sem.at[c, k - 1],
            recv_sem=recv_sem.at[c, k - 1],
            device_id=chan_peer(k),
            device_id_type=pl.DeviceIdType.MESH,
        )

    def local(c):
        start, size = span(c)
        return pltpu.make_async_copy(
            s_ref.at[:, :, pl.ds(me * total + start, size)],
            r_ref.at[:, :, pl.ds(start, size), mine],
            own_sem.at[c],
        )

    twin = here + 1 - 2 * lax.rem(here, 2)
    over = lax.rem(here + 2, ranges)
    far = lax.rem(twin + 2, ranges)

    def summand(c, k):
        source = z_ref.at[pl.ds(c * chunk + (twin, far)[k] * part, part)] if k < 2 else t_ref.at[c]
        return pltpu.make_async_remote_copy(
            src_ref=source,
            dst_ref=got_ref.at[c, k],
            send_sem=zsend_sem.at[c, k],
            recv_sem=zrecv_sem.at[c, k],
            device_id={"range": twin if k < 2 else over},
            device_id_type=pl.DeviceIdType.MESH,
        )

    for reach in (range(1, group), range(group, owners)):
        for c in range(count):
            for k in reach:
                outgoing(c, k).start()
    for c in range(count):
        local(c).start()

    rows = lax.broadcasted_iota(jnp.int32, (order, order), 0)
    cols = lax.broadcasted_iota(jnp.int32, (order, order), 1)
    upper = rows <= cols

    def relay(c):
        summand(c, 1).wait_recv()
        t_ref[c] = z_ref[pl.ds(c * chunk + over * part, part)] + got_ref[c, 1]
        summand(c, 0).wait_recv()
        share_ref[pl.ds(c * part, part)] = (
            z_ref[pl.ds(c * chunk + here * part, part)] + got_ref[c, 0]
        )
        summand(c, 2).start()

    def collect(c):
        summand(c, 2).wait_recv()
        span = pl.ds(c * part, part)
        share_ref[span] = share_ref[span] + got_ref[c, 2]

    for c in range(count):
        for k in range(1, owners):
            outgoing(c, k).wait_recv()
        local(c).wait()

        @pl.loop(0, chunk)
        def _(i):
            j = c * chunk + i
            pieces = [
                [r_ref[p, t, pl.ds(j, 2)].reshape(order, LANES) for t in range(tiles)]
                for p in range(2)
            ]
            whole = jnp.concatenate([jnp.concatenate(p, 1) for p in pieces], 0)
            masked = jnp.concatenate(
                [
                    jnp.concatenate([pieces[p][t] * w_ref[j, t] for t in range(tiles)], 1)
                    for p in range(2)
                ],
                0,
            )
            g = dot3(split(masked), split(whole), ((1,), (1,)))
            re = g[:order, :order] + g[order:, order:]
            im = g[:order, order:] - g[order:, :order]
            z_ref[j] = jnp.where(upper, re, im) * scaling

        @pl.loop(0, chunk)
        def _(i):
            j = c * chunk + i
            for p in range(2):
                for t in range(tiles):
                    o_ref[p, j, :, t * LANES : (t + 1) * LANES] = r_ref[p, t, j].astype(BF)

        for k in range(2):
            summand(c, 1 - k).start()
        if c > 0:
            relay(c - 1)
        if c > 1:
            collect(c - 2)
    relay(count - 1)
    for c in range(max(0, count - 2), count):
        collect(c)
    for c in range(count):
        for k in range(1, owners):
            outgoing(c, k).wait_send()
        for k in range(3):
            summand(c, k).wait_send()


def exchange(spectra, weights, scaling, chunk, owners, ranges):
    _, tiles, _, channels, _ = spectra.shape
    total = weights.shape[0]
    full = channels * owners
    order = 2 * full
    count = total // chunk
    part = chunk // ranges
    dma = pltpu.SemaphoreType.DMA
    return pl.pallas_call(
        functools.partial(exchange_kernel, chunk, scaling),
        in_specs=[
            pl.BlockSpec(memory_space=pltpu.SMEM),
            pl.BlockSpec(memory_space=pl.ANY),
        ],
        out_specs=[pl.BlockSpec(memory_space=pltpu.VMEM)] * 2,
        out_shape=[
            jax.ShapeDtypeStruct((count * part, order, order), F32),
            jax.ShapeDtypeStruct((2, total, full, tiles * LANES), BF),
        ],
        scratch_shapes=[
            pltpu.VMEM((2, tiles, total + 1, full, LANES), F32),
            pltpu.VMEM((total, order, order), F32),
            pltpu.VMEM((count, 3, part, order, order), F32),
            pltpu.VMEM((count, part, order, order), F32),
            dma((count,)),
            dma((count, owners - 1)),
            dma((count, owners - 1)),
            dma((count, 3)),
            dma((count, 3)),
        ],
        compiler_params=pltpu.CompilerParams(
            vmem_limit_bytes=VMEM_LIMIT, collective_id=0, has_side_effects=True
        ),
        name="exchange",
    )(weights, spectra)


def factor_kernel(count, order, z_ref, o_ref, re_ref, im_ref, sr_ref, si_ref):
    rows = lax.broadcasted_iota(jnp.int32, (order, order), 0)
    cols = lax.broadcasted_iota(jnp.int32, (order, order), 1)
    lane = lax.broadcasted_iota(jnp.int32, (count, order), 1)

    @pl.loop(0, count)
    def _(b):
        z = z_ref[b]
        re_ref[b] = z
        im_ref[b] = jnp.where(rows < cols, -z.T, 0.0)

    for offset in range(0, order, STRIP):
        for b in range(count):
            sr_ref[pl.ds(b, STRIP, stride=count), :] = re_ref[b, offset : offset + STRIP, :]
            si_ref[pl.ds(b, STRIP, stride=count), :] = im_ref[b, offset : offset + STRIP, :]
        now_r = [sr_ref[i * count : (i + 1) * count, :] for i in range(STRIP)]
        now_i = [si_ref[i * count : (i + 1) * count, :] for i in range(STRIP)]
        for i in range(STRIP):
            k = offset + i
            pivot = jnp.broadcast_to(now_r[i][:, k : k + 1], (count, order))
            root = lax.rsqrt(pivot)
            row_r = jnp.where(lane >= k, now_r[i] * root, 0.0)
            row_i = jnp.where(lane > k, now_i[i] * root, 0.0)
            for j in range(i + 1, STRIP):
                m = offset + j
                cr = jnp.broadcast_to(row_r[:, m : m + 1], (count, order))
                ci = jnp.broadcast_to(row_i[:, m : m + 1], (count, order))
                now_r[j] = now_r[j] - cr * row_r - ci * row_i
                now_i[j] = now_i[j] - cr * row_i + ci * row_r
            sr_ref[i * count : (i + 1) * count, :] = row_r
            si_ref[i * count : (i + 1) * count, :] = row_i
        done = offset + STRIP

        for b in range(count):
            fr = sr_ref[pl.ds(b, STRIP, stride=count), :]
            fi = si_ref[pl.ds(b, STRIP, stride=count), :]
            re_ref[b, offset:done, :] = fr
            im_ref[b, offset:done, :] = fi
            if done < order:
                left = jnp.concatenate([fr, fi], 0)
                right = jnp.concatenate(
                    [jnp.concatenate([fr, fi], 0), jnp.concatenate([fi, -fr], 0)], 1
                )
                lh, ll = split(left)
                rh, rl = split(right)
                update = dot(
                    jnp.concatenate([lh, lh, ll], 0)[:, :],
                    jnp.concatenate([rh, rl, rh], 0),
                    ((0,), (0,)),
                )
                re_ref[b, done:, :] = re_ref[b, done:, :] - update[done:, :order]
                im_ref[b, done:, :] = im_ref[b, done:, :] - update[done:, order:]

    @pl.loop(0, count)
    def _(b):
        o_ref[b] = jnp.where(rows <= cols, re_ref[b], im_ref[b].T)


def make_factor(gram):
    count, order, _ = gram.shape
    return pl.pallas_call(
        functools.partial(factor_kernel, count, order),
        out_shape=jax.ShapeDtypeStruct((count, order, order), F32),
        scratch_shapes=[
            pltpu.VMEM((count, order, order), F32),
            pltpu.VMEM((count, order, order), F32),
            pltpu.VMEM((STRIP * count, order), F32),
            pltpu.VMEM((STRIP * count, order), F32),
        ],
        compiler_params=pltpu.CompilerParams(vmem_limit_bytes=VMEM_LIMIT),
        name="factor",
    )(gram)


def gather_kernel(pieces, p_ref, o_ref, own_sem, send_sem, recv_sem):
    here = lax.axis_index("range")
    twin = here + 1 - 2 * lax.rem(here, 2)
    over = lax.rem(here + 2, 4)
    size = p_ref.shape[0] // pieces

    barrier = pltpu.get_barrier_semaphore()
    for peer in (twin, over):
        pl.semaphore_signal(
            barrier, inc=1, device_id={"range": peer}, device_id_type=pl.DeviceIdType.MESH
        )
    pl.semaphore_wait(barrier, 2)

    def send(kind, q):
        span = pl.ds(q * size, size)
        owner, peer = ((here, over), (here, twin), (over, twin))[kind]
        return pltpu.make_async_remote_copy(
            src_ref=p_ref.at[span] if kind < 2 else o_ref.at[owner, span],
            dst_ref=o_ref.at[owner, span],
            send_sem=send_sem.at[kind, q],
            recv_sem=recv_sem.at[kind, q],
            device_id={"range": peer},
            device_id_type=pl.DeviceIdType.MESH,
        )

    for kind in range(2):
        for q in range(pieces):
            send(kind, q).start()
    own = pltpu.make_async_copy(p_ref, o_ref.at[here], own_sem)
    own.start()
    for q in range(pieces):
        send(0, q).wait_recv()
        send(2, q).start()
    for q in range(pieces):
        send(1, q).wait_recv()
        send(2, q).wait_recv()
        for kind in range(3):
            send(kind, q).wait_send()
    own.wait()


def gather(packed):
    pieces = math.gcd(packed.shape[0], 4)
    dma = pltpu.SemaphoreType.DMA
    return pl.pallas_call(
        functools.partial(gather_kernel, pieces),
        in_specs=[pl.BlockSpec(memory_space=pltpu.VMEM)],
        out_specs=pl.BlockSpec(memory_space=pl.ANY),
        out_shape=jax.ShapeDtypeStruct((4,) + packed.shape, F32),
        scratch_shapes=[dma, dma((3, pieces)), dma((3, pieces))],
        compiler_params=pltpu.CompilerParams(collective_id=1, has_side_effects=True),
        name="gather",
    )(packed)


def unpack_kernel(p_ref, o_ref):
    order = p_ref.shape[-1]
    rows = lax.broadcasted_iota(jnp.int32, (order, order), 0)
    cols = lax.broadcasted_iota(jnp.int32, (order, order), 1)
    for b in range(p_ref.shape[0]):
        z = p_ref[b]
        o_ref[b, 0] = jnp.where(rows <= cols, z, 0.0)
        o_ref[b, 1] = jnp.where(rows < cols, z.T, 0.0)


def unpack_factor(packed, count):
    ranges, share, order, _ = packed.shape
    bins = share // count
    packed = packed.reshape(ranges, count, bins, order, order)
    return pl.pallas_call(
        unpack_kernel,
        grid=(count, ranges),
        in_specs=[
            pl.BlockSpec((None, None, bins, order, order), lambda c, r: (r, c, 0, 0, 0))
        ],
        out_specs=pl.BlockSpec(
            (bins, 2, order, order), lambda c, r: (c * ranges + r, 0, 0, 0)
        ),
        out_shape=jax.ShapeDtypeStruct((ranges * share, 2, order, order), F32),
        name="unpack",
    )(packed)


def on_device(echoes, chirp, train_mask):
    tap_span = chirp.shape[-1] - 1
    _, channels, pulses, gates = echoes.shape
    tiles = gates // LANES
    ranges, owners = lax.axis_size("range"), lax.axis_size("chan")
    total = train_mask.shape[0]
    chunk = total // CHUNKS
    rim = from_behind(echoes[..., :tap_span], "range", -1)
    weights = train_mask.astype(F32)
    scaling = 1.0 / (gates * ranges)
    wrap = int(channels % 8 == 0 and chunk % ranges == 0 and ranges == 4)
    spectra = make_spectra(echoes, rim, chirp, wrap)
    spectra = spectra.reshape(2, tiles, pulses + wrap, channels, LANES)
    if wrap:
        count = CHUNKS
        share, spectra_out = exchange(spectra, weights, scaling, chunk, owners, ranges)
    else:
        count = 1
        turned = lax.all_to_all(spectra, "chan", split_axis=2, concat_axis=3, tiled=True)
        edge = from_behind_2(turned[:, :, :1], "chan", -1)
        bins = math.gcd(total, 8)
        firsts = jnp.concatenate([turned[:, :, bins::bins], edge], 2)
        packed, spectra_out = make_gram(turned, firsts, weights, scaling, bins)
        share = lax.psum_scatter(packed, "range", scatter_dimension=0, tiled=True)
    mine = make_factor(share)
    pooled = gather(mine) if ranges == 4 else lax.all_gather(mine, "range", axis=0)
    factors = unpack_factor(pooled, count)
    return (spectra_out, factors)


def solution(mesh):
    return jax.shard_map(
        on_device,
        mesh=mesh,
        in_specs=(P(None, "chan", None, "range"), P(), P("chan", "range")),
        out_specs=(P(None, "chan", None, "range"), P("chan", None, None, None)),
        check_vma=False,
    )
```
